256 devices in a mesh: region: 8 (over x, core), dom: 32 (over z, y).
Axes of the slice: x: 4, y: 4, z: 8, core: 2. Of those that a mesh axis runs over, the one named last changes fastest.
Arguments:
- x_init: bfloat16 [1048576, 128], P(('region', 'dom')), may hold values from -6 to 6
- tiles: bfloat16 [73728, 128, 128], P(('region', 'dom'))
- tile_row: int32 [73728], P(('region', 'dom')), may hold values from 0 to 31
- tile_col: int32 [73728], P(('region', 'dom')), may hold values from 0 to 63, as said below
- send_list: int32 [256, 4, 8], P(('region', 'dom')), may hold values from 0 to 31, as said below
- send_count: int32 [256, 4], P(('region', 'dom')), may hold values from 1 to 8, as said below
Outputs:
- basis: bfloat16 [1048576, 128], P(('region', 'dom'))
- ritz_matrix: float32 [2, 128, 128], replicated
The draws below stay inside these ranges and needn't reach their ends.
Inputs may be any that keep to these rules, and one draw needn't show every extreme that they name: `send_list`: the 8 entries of one partition and direction are distinct row tiles of that partition. `send_count`: some partition sends 8 row tiles in every direction. `tile_col`: a value 32 + d * 8 + s with d = 0 .. 3 names slot s of the d-th received stack of extended, and s is below the count that this neighbour sends; no value names a stack where the neighbour does not exist.
All inputs are finite; a program needn't handle non-finite values.
Results may differ from the reference program's by a relative error of at most 0.00115.
The reference program's roundings to bfloat16 on the way count: a program that leaves them out, or rounds other values in their place, can miss the bound.
Values may be sent and summed in bfloat16 or wider, within the bound.
No kernel may reach another device: no remote copies, remote signals or barrier semaphores. Data moves between devices by JAX's collectives and lax.ppermute only.
A program may use at most 64 MiB of HBM per device.

```python
import math
import jax
import jax.numpy as jnp
from jax import lax

K = 128
B = 128
RT = 32
NTD = 288
CAP = 8
ITERS = 2
REGIONS = 8
PER_REGION = 32
PARTITIONS = 256
NODES = 1048576


def link_counts(key):
    seeded = jax.random.fold_in(key, 11)
    count_parts = REGIONS * PER_REGION
    counts = jax.random.randint(jax.random.fold_in(seeded, 1), (count_parts, 4), 1, CAP + 1)
    chosen = jax.random.randint(jax.random.fold_in(seeded, 2), (), 0, count_parts - 1)
    part_ids = jnp.arange(count_parts)[:, None]
    dir_ids = jnp.arange(4)[None, :]
    counts = jnp.where(part_ids == chosen, CAP, counts)
    counts = jnp.where((part_ids == PER_REGION) & (dir_ids == 3), CAP, counts)
    counts = jnp.where((part_ids == count_parts - 1) & (dir_ids == 0), 1, counts)
    return counts.astype(jnp.int32)


def draw_send_count(key, part):
    return link_counts(key)


def draw_send_list(key, part):
    count_parts = REGIONS * PER_REGION
    keys = jax.random.split(jax.random.fold_in(key, 23), count_parts * 4)
    positions = jnp.arange(RT, dtype=jnp.int32)

    def one_list(single, index):
        order = jax.random.permutation(single, RT).astype(jnp.int32)
        first = order[0]
        moved = jnp.where(order == RT - 1, first, jnp.where(positions == 0, RT - 1, order))
        second = moved[1]
        moved = jnp.where(moved == 0, second, jnp.where(positions == 1, 0, moved))
        return jnp.where(index == 0, moved, order)[:CAP]
    lists = jax.vmap(one_list)(keys, jnp.arange(count_parts * 4, dtype=jnp.int32))
    return lists.reshape(count_parts, 4, CAP).astype(jnp.int32)


def draw_tile_col(key, part):
    count_parts = REGIONS * PER_REGION
    counts = link_counts(key).reshape(REGIONS, PER_REGION, 4)
    zero_dom = jnp.zeros((REGIONS, 1), jnp.int32)
    zero_region = jnp.zeros((1, PER_REGION), jnp.int32)
    live_lower_dom = jnp.concatenate([zero_dom, counts[:, :-1, 0]], axis=1)
    live_upper_dom = jnp.concatenate([counts[:, 1:, 1], zero_dom], axis=1)
    live_lower_region = jnp.concatenate([zero_region, counts[:-1, :, 2]], axis=0)
    live_upper_region = jnp.concatenate([counts[1:, :, 3], zero_region], axis=0)
    live_counts = jnp.stack([live_lower_dom, live_upper_dom, live_lower_region, live_upper_region], axis=-1)
    live_counts = live_counts.reshape(count_parts, 4)
    seeded = jax.random.fold_in(key, 37)
    category = jax.random.randint(jax.random.fold_in(seeded, 1), (count_parts, NTD), 0, 8)
    own_tile = jax.random.randint(jax.random.fold_in(seeded, 2), (count_parts, NTD), 0, RT)
    slot_draw = jax.random.randint(jax.random.fold_in(seeded, 3), (count_parts, NTD), 0, 65520)
    direction = jnp.clip(category - 4, 0, 3)
    available = jnp.take_along_axis(live_counts, direction, axis=1)
    slot_index = slot_draw % jnp.maximum(available, 1)
    remote = RT + direction * CAP + slot_index
    use_remote = (category >= 4) & (available > 0)
    result = jnp.where(use_remote, remote, own_tile)
    part_ids = jnp.arange(count_parts)[:, None]
    tile_ids = jnp.arange(NTD)[None, :]
    result = jnp.where((part_ids == 0) & (tile_ids == 0), RT + 4 * CAP - 1, result)
    result = jnp.where((part_ids == 0) & (tile_ids == 1), 0, result)
    return result.reshape(count_parts * NTD).astype(jnp.int32)


def draw_tiles(key, part):
    count_parts = REGIONS * PER_REGION
    fan_total = B * NTD // RT
    seeded = jax.random.fold_in(key, 53)
    rising = 3.0 ** (jnp.arange(count_parts, dtype=jnp.float32) / max(count_parts - 1, 1))
    values = jax.random.normal(seeded, (count_parts, NTD, B, B), jnp.float32)
    values = values * (rising[:, None, None, None] / math.sqrt(fan_total))
    return values.reshape(count_parts * NTD, B, B).astype(jnp.bfloat16)


def plant(array, rng, least, high):
    spot = [jax.random.randint(jax.random.fold_in(rng, axis), (), 0, length) for axis, length in enumerate(array.shape)]
    main_axis = array.shape.index(max(array.shape))
    beside = spot[:main_axis] + [(spot[main_axis] + 1) % array.shape[main_axis]] + spot[main_axis + 1:]
    return array.at[tuple(spot)].set(least).at[tuple(beside)].set(high)


def block_scale(rng, dims, shards, least, high):
    gain = 1.0
    for axis_at, blocks in shards:
        steps = jax.random.uniform(jax.random.fold_in(jax.random.fold_in(rng, 6), axis_at), (blocks,), jnp.float32, least / len(shards), high / len(shards))
        gain = gain * jnp.repeat(jnp.exp(steps), dims[axis_at] // blocks).reshape((-1,) + (1,) * (len(dims) - 1 - axis_at))
    return gain


def scatter_about(rng, extent, spread, limit, cuts=(), kind=jnp.bfloat16):
    array = spread * jax.random.normal(rng, extent, jnp.float32)
    if cuts:
        array = array * block_scale(rng, extent, cuts, -0.22, 0.18)
    return jnp.clip(array, -limit, limit).astype(kind)


def setup_inputs(seed: int = 0) -> dict:
    key_list = jax.random.split(jax.random.key(seed), 7)
    x_init = scatter_about(key_list[0], (NODES, K), 1.0, 6.0, ((0, 256),))
    tiles = draw_tiles(jax.random.fold_in(key_list[6], 71), 0)
    tile_row = plant(jax.random.randint(key_list[2], (PARTITIONS * NTD,), 0, RT), jax.random.fold_in(key_list[2], 1), 0, RT - 1).astype(jnp.int32)
    tile_col = draw_tile_col(jax.random.fold_in(key_list[6], 71), 0)
    send_list = draw_send_list(jax.random.fold_in(key_list[6], 71), 0)
    send_count = draw_send_count(jax.random.fold_in(key_list[6], 71), 0)
    return dict(x_init=x_init, tiles=tiles, tile_row=tile_row, tile_col=tile_col, send_list=send_list, send_count=send_count)


def gram_of(current, node_total):
    return jnp.dot(current.T.astype(jnp.float32), current.astype(jnp.float32), preferred_element_type=jnp.float32) / node_total

def apply_graph(basis, tiles, tile_row, tile_col, send_list, send_count):
    count_parts = PARTITIONS
    blocks = basis.reshape(count_parts, RT, B, K)
    slots = jnp.arange(CAP, dtype=jnp.int32)
    live_slot = slots[None, None, :] < send_count[:, :, None]
    picked = jax.vmap(lambda own_tiles, row_list: own_tiles[row_list])(blocks, send_list)
    sends = jnp.where(live_slot[:, :, :, None, None], picked, jnp.zeros_like(picked))
    grid = sends.reshape(REGIONS, PER_REGION, 4, CAP, B, K)
    zero_dom = jnp.zeros_like(grid[:, :1, 0])
    from_lower_dom = jnp.concatenate([zero_dom, grid[:, :-1, 0]], axis=1)
    from_upper_dom = jnp.concatenate([grid[:, 1:, 1], zero_dom], axis=1)
    zero_region = jnp.zeros_like(grid[:1, :, 2])
    from_lower_region = jnp.concatenate([zero_region, grid[:-1, :, 2]], axis=0)
    from_upper_region = jnp.concatenate([grid[1:, :, 3], zero_region], axis=0)
    received = jnp.stack([from_lower_dom, from_upper_dom, from_lower_region, from_upper_region], axis=2)
    received = received.reshape(count_parts, 4 * CAP, B, K)

    def one_part(pieces):
        own_tiles, incoming, part_tiles, part_rows, part_cols = pieces
        extended = jnp.concatenate([own_tiles, incoming], axis=0)
        gathered = extended[part_cols].astype(jnp.float32)
        products = jnp.einsum('tij,tjk->tik', part_tiles.astype(jnp.float32), gathered, precision=lax.Precision.HIGHEST)
        return jax.ops.segment_sum(products, part_rows, num_segments=RT)
    applied = lax.map(one_part, (blocks, received, tiles.reshape(count_parts, NTD, B, B), tile_row.reshape(count_parts, NTD), tile_col.reshape(count_parts, NTD)))
    return applied.reshape(count_parts * RT * B, K)

def reference(x_init, tiles, tile_row, tile_col, send_list, send_count):
    node_total = x_init.shape[0]
    current = x_init
    gram = gram_of(current, node_total)
    identity = jnp.eye(K, dtype=jnp.float32)
    rayleigh_list = []
    basis = x_init
    for iteration in range(ITERS):
        factor = jnp.linalg.cholesky(gram)
        inverse = lax.linalg.triangular_solve(factor, identity, left_side=True, lower=True)
        basis = jnp.dot(current.astype(jnp.float32), inverse.T, precision=lax.Precision.HIGHEST).astype(jnp.bfloat16)
        applied = apply_graph(basis, tiles, tile_row, tile_col, send_list, send_count)
        rayleigh = jnp.dot(basis.astype(jnp.float32).T, applied, precision=lax.Precision.HIGHEST) / math.sqrt(node_total)
        rayleigh_list.append(rayleigh)
        current = applied.astype(jnp.bfloat16)
        if iteration + 1 < ITERS:
            gram = gram_of(current, node_total)
    return (basis, jnp.stack(rayleigh_list))
```

```python
import functools
import math

import jax
import jax.numpy as jnp
from jax import lax
from jax.experimental import pallas as pl
from jax.experimental.pallas import tpu as pltpu
from jax.sharding import PartitionSpec as P

ITERS = 2
UNROLL = 4
F32 = jnp.float32
BF16 = jnp.bfloat16
AXES = ("region", "dom")
PHASES = (("region", (2, 4, 6)), ("dom", (1, 2, 3)), ("dom", (4,)), ("dom", (8, 16, 24)))


def shifted(block, axis, distance):
    devices = range(lax.axis_size(axis))
    route = [(i - distance, i) for i in devices if i - distance in devices]
    return lax.ppermute(block, axis, route)


def partner(block, axis, mask):
    return lax.ppermute(block, axis, [(i, i ^ mask) for i in range(lax.axis_size(axis))])


def exchange_sum(block, axis, masks):
    parts = [block] + [partner(block, axis, mask) for mask in masks]
    while len(parts) > 1:
        parts = [a + b for a, b in zip(parts[::2], parts[1::2])]
    return parts[0]


def sum_everywhere(halves):
    core = lax.axis_index("region") % 2
    mine = lax.dynamic_index_in_dim(halves, core, 0, keepdims=False)
    other = lax.dynamic_index_in_dim(halves, 1 - core, 0, keepdims=False)
    part = mine + partner(other, "region", 1)
    for axis, masks in PHASES:
        part = exchange_sum(part, axis, masks)
    twin = partner(part, "region", 1)
    return jnp.stack([jnp.where(core == 0, part, twin), jnp.where(core == 0, twin, part)])


def reduce_gram(gram):
    size = gram.shape[0]
    return sum_everywhere(gram.reshape(2, size // 2, size)).reshape(size, size)


def pair_table(tile_row, tile_col, row_tiles):
    count = tile_row.shape[0]
    slots = -(-((count + row_tiles + 1) // 2) // UNROLL) * UNROLL
    ids = jnp.arange(count, dtype=jnp.int32)
    rows = jnp.arange(row_tiles, dtype=jnp.int32)
    same = tile_row[:, None] == tile_row[None, :]
    rank = jnp.sum(jnp.where(same & (ids[None, :] < ids[:, None]), 1, 0), axis=1)
    total = jnp.sum(jnp.where(tile_row[None, :] == rows[:, None], 1, 0), axis=1)
    pairs = (total + 1) // 2
    first = jnp.sum(jnp.where(rows[None, :] < rows[:, None], pairs[None, :], 0), axis=1)
    start = jnp.sum(jnp.where(tile_row[:, None] == rows[None, :], first[None, :], 0), axis=1)
    slot = start + rank // 2
    half = rank % 2
    slot_ids = jnp.arange(slots, dtype=jnp.int32)
    at_a = (slot[None, :] == slot_ids[:, None]) & (half[None, :] == 0)
    at_b = (slot[None, :] == slot_ids[:, None]) & (half[None, :] == 1)

    def pick(at, values):
        return jnp.sum(jnp.where(at, values[None, :], 0), axis=1)

    tile_a = count + pick(at_a, ids - count)
    tile_b = count + pick(at_b, ids - count)
    return jnp.stack(
        [tile_a, tile_b, pick(at_a, tile_col), pick(at_b, tile_col), pick(at_a, tile_row)]
    )


def split3(value):
    hi = value.astype(BF16)
    rest = value - hi.astype(F32)
    mid = rest.astype(BF16)
    return hi, mid, (rest - mid.astype(F32)).astype(BF16)


def dot_t(a, b):
    return lax.dot_general(a, b, (((0,), (0,)), ((), ())), preferred_element_type=F32)


def invert_factor(gram):
    size = gram.shape[0]
    blocks = [gram[8 * i : 8 * i + 8, :] for i in range(size // 8)]
    lane = lax.broadcasted_iota(jnp.int32, (8, size), 1)
    sub = lax.broadcasted_iota(jnp.int32, (8, size), 0)
    scales = []
    for k in range(size):
        own, at = k // 8, k % 8
        row = blocks[own][at : at + 1, :]
        pivot = row[:, k : k + 1]
        scales.append(lax.rsqrt(pivot))
        inv = 1.0 / pivot
        here = lane == k
        row = jnp.broadcast_to(row * inv, (8, size))
        row = jnp.where(here, jnp.broadcast_to(inv, (8, size)), row)
        for j in range(own, size // 8):
            if j == own and at == 7:
                continue
            old = blocks[j]
            col = jnp.broadcast_to(old[:, k : k + 1], (8, size))
            new = jnp.where(here, 0.0, old) - col * row
            blocks[j] = jnp.where(sub > at, new, old) if j == own else new
    out = []
    for i in range(size // 8):
        scale = jnp.concatenate(
            [jnp.broadcast_to(scales[8 * i + s], (1, size)) for s in range(8)], axis=0
        )
        keep = lane < sub + 8 * i
        diag = lane == sub + 8 * i
        out.append(jnp.where(diag, scale, jnp.where(keep, blocks[i] * scale, 0.0)))
    return jnp.concatenate(out, axis=0)


def start_kernel(node_total, send_ref, x_ref, gram_ref, *sends):
    size = x_ref.shape[2]
    for d, out in enumerate(sends):
        for s in range(out.shape[0]):
            out[s] = x_ref[send_ref[d, s]]
    total = jnp.zeros((size, size), F32)
    for i in range(0, x_ref.shape[0], 4):
        rows = x_ref[i : i + 4].reshape(-1, size)
        total = total + dot_t(rows, rows)
    gram_ref[...] = total * (1.0 / node_total)


def step_kernel(last, node_total, row_tiles, *refs):
    table, send_ref, gram_ref, own_hbm, h0, h1, h2, h3, tiles_hbm = refs[:9]
    if last:
        basis_out, ray_ref = refs[9:11]
        scratch = refs[11:]
    else:
        gram_out, ray_ref = refs[9:11]
        current_out = refs[11]
        sends = refs[12:16]
        scratch = refs[16:]
    cur, ext, acc, tiles, in_sems, tile_sem = scratch
    count = tiles_hbm.shape[0]
    size = gram_ref.shape[0]
    cap = h0.shape[0]
    copies = [pltpu.make_async_copy(own_hbm, cur.at[pl.ds(0, row_tiles)], in_sems.at[0])]
    for d, h in enumerate((h0, h1, h2, h3)):
        copies.append(
            pltpu.make_async_copy(h, cur.at[pl.ds(row_tiles + d * cap, cap)], in_sems.at[1 + d])
        )
    for copy in copies:
        copy.start()
    tile_copy = pltpu.make_async_copy(tiles_hbm, tiles.at[pl.ds(0, count)], tile_sem)
    tile_copy.start()
    tiles[count] = jnp.zeros((size, size), BF16)

    def clear(i, carry):
        acc[i] = jnp.zeros((size, size), F32)
        return carry

    lax.fori_loop(0, row_tiles, clear, 0)
    weight = invert_factor(gram_ref[...]).T
    hi, mid, lo = split3(weight)
    high = jnp.concatenate([hi, mid], axis=0)
    for copy in copies:
        copy.wait()

    def form(i, carry):
        rows = cur[pl.ds(2 * i, 2)].reshape(2 * size, size)
        twice = jnp.concatenate([rows, rows], axis=1)
        value = jnp.dot(twice, high, preferred_element_type=F32) + jnp.dot(
            rows, lo, preferred_element_type=F32
        )
        ext[pl.ds(2 * i, 2)] = value.astype(BF16).reshape(2, size, size)
        return carry

    lax.fori_loop(0, (row_tiles + 4 * cap) // 2, form, 0)
    tile_copy.wait()

    def products(i, carry):
        values = []
        for u in range(UNROLL):
            p = i * UNROLL + u
            left = jnp.concatenate([tiles[table[0, p]], tiles[table[1, p]]], axis=1)
            right = jnp.concatenate([ext[table[2, p]], ext[table[3, p]]], axis=0)
            values.append(jnp.dot(left, right, preferred_element_type=F32))
        for u in range(UNROLL):
            row = table[4, i * UNROLL + u]
            acc[row] = acc[row] + values[u]
        return carry

    lax.fori_loop(0, table.shape[1] // UNROLL, products, 0)

    if last:
        basis_out[...] = ext[0:row_tiles]

    def reduce_rows(i, carry):
        main, rest = carry
        basis = ext[pl.ds(2 * i, 2)].reshape(2 * size, size)
        hi, mid, lo = split3(acc[pl.ds(2 * i, 2)].reshape(2 * size, size))
        right = jnp.concatenate([hi, mid], axis=1)
        if last:
            left = basis
        else:
            current_out[pl.ds(2 * i, 2)] = hi.reshape(2, size, size)
            left = jnp.concatenate([basis, hi], axis=1)
        return main + dot_t(left, right), rest + dot_t(basis, lo)

    width = size if last else 2 * size
    main, rest = lax.fori_loop(
        0,
        row_tiles // 2,
        reduce_rows,
        (jnp.zeros((width, 2 * size), F32), jnp.zeros((size, size), F32)),
    )
    ray = main[:size, :size] + (main[:size, size:] + rest)
    ray_ref[...] = ray * (1.0 / math.sqrt(node_total))
    if not last:
        gram_out[...] = main[size:, :size] * (1.0 / node_total)
        for d, out in enumerate(sends):
            for s in range(cap):
                out[s] = current_out[send_ref[d, s]]


SMEM = pl.BlockSpec(memory_space=pltpu.SMEM)
VMEM = pl.BlockSpec(memory_space=pltpu.VMEM)
ANY = pl.BlockSpec(memory_space=pl.ANY)


def shards(x_init, tiles, tile_row, tile_col, send_list, send_count):
    row_count, vectors = x_init.shape
    size = tiles.shape[1]
    row_tiles = row_count // size
    cap = send_list.shape[2]
    node_total = row_count * lax.axis_size("region") * lax.axis_size("dom")
    send_rows = send_list[0]
    table = pair_table(tile_row, tile_col, row_tiles)
    square = jax.ShapeDtypeStruct((size, vectors), F32)
    block = jax.ShapeDtypeStruct((row_tiles, size, vectors), BF16)
    boundary = [jax.ShapeDtypeStruct((cap, size, vectors), BF16)] * 4

    current = x_init.reshape(row_tiles, size, vectors)
    gram, *sends = pl.pallas_call(
        functools.partial(start_kernel, node_total),
        name="start",
        out_shape=[square] + boundary,
        in_specs=[SMEM, VMEM],
        out_specs=[VMEM] * 5,
    )(send_rows, current)
    rays = []
    for iteration in range(ITERS):
        last = iteration + 1 == ITERS
        halo = [
            shifted(sends[0], "dom", 1),
            shifted(sends[1], "dom", -1),
            shifted(sends[2], "region", 1),
            shifted(sends[3], "region", -1),
        ]
        gram = reduce_gram(gram)
        out_shape = [block, square] if last else [square, square, block] + boundary
        outs = pl.pallas_call(
            functools.partial(step_kernel, last, node_total, row_tiles),
            name="finish" if last else "step",
            out_shape=out_shape,
            in_specs=[SMEM, SMEM, VMEM] + [ANY] * 6,
            out_specs=[VMEM] * len(out_shape),
            scratch_shapes=[
                pltpu.VMEM((row_tiles + 4 * cap, size, vectors), BF16),
                pltpu.VMEM((row_tiles + 4 * cap, size, vectors), BF16),
                pltpu.VMEM((row_tiles, size, vectors), F32),
                pltpu.VMEM((tiles.shape[0] + 1, size, size), BF16),
                pltpu.SemaphoreType.DMA((5,)),
                pltpu.SemaphoreType.DMA,
            ],
        )(table, send_rows, gram, current, *halo, tiles)
        if last:
            basis, ray = outs
        else:
            gram, ray, current, *sends = outs
        rays.append(ray)
    return basis.reshape(row_count, vectors), sum_everywhere(jnp.stack(rays))


def solution(mesh):
    in_specs = (
        P(AXES, None),
        P(AXES, None, None),
        P(AXES),
        P(AXES),
        P(AXES, None, None),
        P(AXES, None),
    )
    out_specs = (P(AXES, None), P())
    return jax.shard_map(shards, mesh=mesh, in_specs=in_specs, out_specs=out_specs, check_vma=False)
```

```python
import functools
import math

import jax
import jax.numpy as jnp
from jax import lax
from jax.experimental import pallas as pl
from jax.experimental.pallas import tpu as pltpu
from jax.sharding import PartitionSpec as P


ITERS = 2
UNROLL = 32
FORM = 16
REDUCE = 8
F32 = jnp.float32
BF16 = jnp.bfloat16
AXES = ("region", "dom")
PHASES = (("region", (2, 4, 6)), ("dom", (1, 2, 3)), ("dom", (4,)), ("dom", (8, 16, 24)))
EDGES = (("dom", 0), ("dom", 1), ("region", 1), ("region", 0))


def edge_pairs(size, parity):
    pairs = [(i, i + 1) for i in range(parity, size - 1, 2)]
    return pairs + [(j, i) for i, j in pairs]


def sends_up(parity, index):
    return (index % 2) == parity


def partner(block, axis, mask):
    return lax.ppermute(block, axis, [(i, i ^ mask) for i in range(lax.axis_size(axis))])


def exchange_sum(block, axis, masks):
    parts = [block] + [partner(block, axis, mask) for mask in masks]
    while len(parts) > 1:
        parts = [a + b for a, b in zip(parts[::2], parts[1::2])]
    return parts[0]


def sum_chips(part):
    for axis, masks in PHASES:
        part = exchange_sum(part, axis, masks)
    return part


def pair_table(tile_row, tile_col, row_tiles):
    count = tile_row.shape[0]
    slots = -(-((count + row_tiles + 1) // 2) // UNROLL) * UNROLL
    ids = jnp.arange(count, dtype=jnp.int32)
    rows = jnp.arange(row_tiles, dtype=jnp.int32)
    same = tile_row[:, None] == tile_row[None, :]
    rank = jnp.sum(jnp.where(same & (ids[None, :] < ids[:, None]), 1, 0), axis=1)
    total = jnp.sum(jnp.where(tile_row[None, :] == rows[:, None], 1, 0), axis=1)
    pairs = (total + 1) // 2
    first = jnp.sum(jnp.where(rows[None, :] < rows[:, None], pairs[None, :], 0), axis=1)
    start = jnp.sum(jnp.where(tile_row[:, None] == rows[None, :], first[None, :], 0), axis=1)
    slot = start + rank // 2
    half = rank % 2
    slot_ids = jnp.arange(slots, dtype=jnp.int32)
    at_a = (slot[None, :] == slot_ids[:, None]) & (half[None, :] == 0)
    at_b = (slot[None, :] == slot_ids[:, None]) & (half[None, :] == 1)

    def pick(at, values):
        return jnp.sum(jnp.where(at, values[None, :], 0), axis=1)

    tile_a = count + pick(at_a, ids - count)
    tile_b = count + pick(at_b, ids - count)
    return jnp.stack(
        [tile_a, tile_b, pick(at_a, tile_col), pick(at_b, tile_col), pick(at_a, tile_row)]
    )


def split3(value):
    hi = value.astype(BF16)
    rest = value - hi.astype(F32)
    mid = rest.astype(BF16)
    return hi, mid, (rest - mid.astype(F32)).astype(BF16)


def dot_t(a, b):
    return lax.dot_general(a, b, (((0,), (0,)), ((), ())), preferred_element_type=F32)


def invert_factor(gram):
    size = gram.shape[0]
    count = size // 8
    blocks = [gram[8 * i : 8 * i + 8, :] for i in range(count)]
    full = (8, size)
    lane = lax.broadcasted_iota(jnp.int32, full, 1)
    sub = lax.broadcasted_iota(jnp.int32, full, 0)

    def column(block, k):
        return jnp.broadcast_to(block[:, k : k + 1], full)

    def row(block, k):
        return jnp.broadcast_to(block[k : k + 1, :], full)

    out = []
    for b in range(count):
        base = 8 * b
        block = blocks[b]
        inside = (lane >= base) & (lane < base + 8)
        cols = [column(block, base + j) for j in range(8)]
        d = [[row(cols[j], i) for j in range(i + 1)] for i in range(8)]
        low = [[None] * 8 for _ in range(8)]
        inv = []
        for k in range(8):
            inv.append(1.0 / d[k][k])
            for i in range(k + 1, 8):
                low[i][k] = d[i][k] * inv[k]
            for i in range(k + 1, 8):
                for j in range(k + 1, i + 1):
                    d[i][j] = d[i][j] - low[i][k] * d[j][k]
        new = []
        for k in range(8):
            value = jnp.where(inside, jnp.where(lane == base + k, 1.0, 0.0), row(block, k))
            for j in range(k):
                value = value - low[k][j] * new[j]
            new.append(value)
        result = jnp.zeros(full, F32)
        for k in range(8):
            scaled = jnp.where(lane <= base + k, new[k] * lax.rsqrt(d[k][k]), 0.0)
            result = jnp.where(sub == k, scaled, result)
        out.append(result)
        for i in range(b + 1, count):
            old = blocks[i]
            value = jnp.where(inside, 0.0, old)
            terms = []
            for k in range(8):
                t = column(old, base + k)
                for j in range(k):
                    t = t - low[k][j] * terms[j]
                terms.append(t)
            for k in range(8):
                value = value - (terms[k] * inv[k]) * new[k]
            blocks[i] = value
    return jnp.concatenate(out, axis=0)


def pack_square(square):
    half = square.shape[0] // 2
    row = lax.broadcasted_iota(jnp.int32, (half, half), 0)
    col = lax.broadcasted_iota(jnp.int32, (half, half), 1)
    second = square[half:, half:]
    right = jnp.where(row >= col, square[:half, :half], second)
    diag = jnp.sum(jnp.where(row == col, second, 0.0), axis=0, keepdims=True)
    diag = jnp.broadcast_to(diag, (8, half))
    top = jnp.concatenate([square[half:, :half], right], axis=1)
    return jnp.concatenate([top, jnp.concatenate([diag, diag], axis=1)], axis=0)


def unpack_square(packed):
    half = packed.shape[1] // 2
    row = lax.broadcasted_iota(jnp.int32, (half, half), 0)
    col = lax.broadcasted_iota(jnp.int32, (half, half), 1)
    corner = packed[:half, :half]
    right = packed[:half, half:]
    turned = right.T
    diag = jnp.broadcast_to(packed[half : half + 1, :half], (half, half))
    first = jnp.where(row >= col, right, turned)
    second = jnp.where(row < col, right, jnp.where(row > col, turned, diag))
    return jnp.concatenate(
        [jnp.concatenate([first, corner.T], axis=1), jnp.concatenate([corner, second], axis=1)],
        axis=0,
    )


def gather_sends(send_ref, current, sends):
    index = {"region": lax.axis_index("region"), "dom": lax.axis_index("dom")}
    for (axis, parity), out in zip(EDGES, sends):
        base = 0 if axis == "dom" else 2
        way = base + jnp.where(sends_up(parity, index[axis]), 0, 1)
        for s in range(out.shape[0]):
            out[s] = current[send_ref[way, s]]


def start_kernel(node_total, send_ref, x_ref, gram_ref, *sends):
    size = x_ref.shape[2]
    gather_sends(send_ref, x_ref, sends)
    total = jnp.zeros((size, size), F32)
    for i in range(0, x_ref.shape[0], 8):
        rows = x_ref[i : i + 8].reshape(-1, size)
        total = total + dot_t(rows, rows)
    gram_ref[...] = pack_square(total * (1.0 / node_total))


def step_kernel(last, node_total, *refs):
    table, send_ref, gram_ref, own = refs[:4]
    halos = refs[4:8]
    tiles_hbm = refs[8]
    if last:
        ray_in, basis_out, mine_ref, other_ref = refs[9:13]
        scratch = refs[13:]
    else:
        gram_out, ray_ref, current_out = refs[9:12]
        sends = refs[12:16]
        scratch = refs[16:]
    ext, acc, tiles, out_sem, tile_sem = scratch
    count = tiles_hbm.shape[0]
    size = tiles_hbm.shape[1]
    row_tiles = own.shape[0]
    cap = halos[0].shape[0]
    tile_copy = pltpu.make_async_copy(tiles_hbm, tiles.at[pl.ds(0, count)], tile_sem)
    tile_copy.start()
    tiles[count] = jnp.zeros((size, size), BF16)

    def clear(i, carry):
        acc[pl.ds(4 * i, 4)] = jnp.zeros((4, size, size), F32)
        return carry

    lax.fori_loop(0, row_tiles // 4, clear, 0)
    weight = invert_factor(unpack_square(gram_ref[...])).T
    hi, mid, lo = split3(weight)

    def form(rows):
        count = rows.shape[0]
        rows = rows.reshape(count * size, size)
        value = jnp.dot(rows, hi, preferred_element_type=F32) + (
            jnp.dot(rows, mid, preferred_element_type=F32)
            + jnp.dot(rows, lo, preferred_element_type=F32)
        )
        return value.astype(BF16).reshape(count, size, size)

    def form_own(i, carry):
        ext[pl.ds(FORM * i, FORM)] = form(own[pl.ds(FORM * i, FORM)])
        return carry

    lax.fori_loop(0, row_tiles // FORM, form_own, 0)
    if last:
        basis_copy = pltpu.make_async_copy(ext.at[pl.ds(0, row_tiles)], basis_out, out_sem)
        basis_copy.start()
    index = {"region": lax.axis_index("region"), "dom": lax.axis_index("dom")}
    for (axis, parity), halo in zip(EDGES, halos):
        stack = (0 if axis == "dom" else 2) + jnp.where(sends_up(parity, index[axis]), 1, 0)
        ext[pl.ds(row_tiles + stack * cap, cap)] = form(halo[...])
    tile_copy.wait()

    def products(i, carry):
        values = []
        for u in range(UNROLL):
            p = i * UNROLL + u
            left = jnp.concatenate([tiles[table[0, p]], tiles[table[1, p]]], axis=1)
            right = jnp.concatenate([ext[table[2, p]], ext[table[3, p]]], axis=0)
            values.append(jnp.dot(left, right, preferred_element_type=F32))
        for u in range(UNROLL):
            row = table[4, i * UNROLL + u]
            acc[row] = acc[row] + values[u]
        return carry

    lax.fori_loop(0, table.shape[1] // UNROLL, products, 0)

    def reduce_rows(i, carry):
        main, rest = carry
        basis = ext[pl.ds(REDUCE * i, REDUCE)].reshape(REDUCE * size, size)
        hi, mid, lo = split3(acc[pl.ds(REDUCE * i, REDUCE)].reshape(REDUCE * size, size))
        right = jnp.concatenate([hi, mid], axis=1)
        if last:
            left = basis
        else:
            current_out[pl.ds(REDUCE * i, REDUCE)] = hi.reshape(REDUCE, size, size)
            left = jnp.concatenate([basis, hi], axis=1)
        return main + dot_t(left, right), rest + dot_t(basis, lo)

    width = size if last else 2 * size
    main, rest = lax.fori_loop(
        0,
        row_tiles // REDUCE,
        reduce_rows,
        (jnp.zeros((width, 2 * size), F32), jnp.zeros((size, size), F32)),
    )
    ray = main[:size, :size] + (main[:size, size:] + rest)
    ray = ray * (1.0 / math.sqrt(node_total))
    if last:
        second = lax.axis_index("region") % 2 == 1
        mine_ref[...] = jnp.where(second, ray, ray_in[...])
        other_ref[...] = jnp.where(second, ray_in[...], ray)
        basis_copy.wait()
    else:
        ray_ref[...] = ray
        gram_out[...] = pack_square(main[size:, :size] * (1.0 / node_total))
        gather_sends(send_ref, current_out, sends)


SMEM = pl.BlockSpec(memory_space=pltpu.SMEM)
VMEM = pl.BlockSpec(memory_space=pltpu.VMEM)
ANY = pl.BlockSpec(memory_space=pl.ANY)


def near(value):
    return pltpu.with_memory_space_constraint(value, pltpu.VMEM)


def shards(x_init, tiles, tile_row, tile_col, send_list, send_count):
    row_count, vectors = x_init.shape
    size = tiles.shape[1]
    row_tiles = row_count // size
    cap = send_list.shape[2]
    node_total = row_count * lax.axis_size("region") * lax.axis_size("dom")
    send_rows = send_list[0]
    square = pltpu.VMEM((size, vectors), F32)
    packed = pltpu.VMEM((size // 2 + 8, vectors), F32)
    block = pltpu.VMEM((row_tiles, size, vectors), BF16)
    boundary = [pltpu.VMEM((cap, size, vectors), BF16)] * 4

    current = x_init.reshape(row_tiles, size, vectors)
    gram, *sends = pl.pallas_call(
        functools.partial(start_kernel, node_total),
        name="start",
        out_shape=[packed] + boundary,
        in_specs=[SMEM, VMEM],
        out_specs=[VMEM] * 5,
        compiler_params=pltpu.CompilerParams(vmem_limit_bytes=16 << 20),
    )(send_rows, current)
    for iteration in range(ITERS):
        last = iteration + 1 == ITERS
        gram = exchange_sum(gram, "region", (1,))
        if iteration == 0:
            gram, tile_row, tile_col = lax.optimization_barrier((gram, tile_row, tile_col))
            table = pair_table(tile_row, tile_col, row_tiles)
        gram, sends = lax.optimization_barrier((gram, sends))
        halos = []
        for (axis, parity), send in zip(EDGES, sends):
            halos.append(
                lax.ppermute(send, axis, edge_pairs(lax.axis_size(axis), parity))
            )
        gram = sum_chips(gram)
        args = [table, send_rows, near(gram), near(current)] + [near(h) for h in halos] + [tiles]
        in_specs = [SMEM, SMEM] + [VMEM] * 6 + [ANY]
        out_shape = [square, packed, block] + boundary
        out_specs = [VMEM] * 7
        if last:
            args.append(near(ray))
            in_specs.append(VMEM)
            out_shape = [jax.ShapeDtypeStruct((row_tiles, size, vectors), BF16), square, square]
            out_specs = [ANY, VMEM, VMEM]
        else:
            out_shape = [packed, square, block] + boundary
        outs = pl.pallas_call(
            functools.partial(step_kernel, last, node_total),
            name="finish" if last else "step",
            out_shape=out_shape,
            in_specs=in_specs,
            out_specs=out_specs,
            scratch_shapes=[
                pltpu.VMEM((row_tiles + 4 * cap, size, vectors), BF16),
                pltpu.VMEM((row_tiles, size, vectors), F32),
                pltpu.VMEM((tiles.shape[0] + 1, size, size), BF16),
                pltpu.SemaphoreType.DMA,
                pltpu.SemaphoreType.DMA,
            ],
            compiler_params=pltpu.CompilerParams(vmem_limit_bytes=40 << 20),
        )(*args)
        if last:
            basis, mine, other = outs
        else:
            gram, ray, current, *sends = outs
    part = sum_chips(mine + partner(other, "region", 1))
    twin = partner(part, "region", 1)
    first = lax.axis_index("region") % 2 == 0
    ritz = jnp.stack([jnp.where(first, part, twin), jnp.where(first, twin, part)])
    return basis.reshape(row_count, vectors), ritz


def solution(mesh):
    in_specs = (
        P(AXES, None),
        P(AXES, None, None),
        P(AXES),
        P(AXES),
        P(AXES, None, None),
        P(AXES, None),
    )
    out_specs = (P(AXES, None), P())
    return jax.shard_map(shards, mesh=mesh, in_specs=in_specs, out_specs=out_specs, check_vma=False)
```
